32 devices in a mesh: rep: 2 (over y), blk: 4 (over z), sect: 2 (over x), sub: 2 (over core).
Axes of the slice: x: 2, y: 2, z: 4, core: 2. Of those that a mesh axis runs over, the one named last changes fastest.
Arguments:
- query_latent: bfloat16 [64, 128, 512], P(('rep', 'blk')), parts along dimension 0, may hold values from -192 to 192
- query_rope: bfloat16 [64, 64, 128], P(('rep', 'blk')), parts along dimension 0, may hold values from -18 to 18
- cache_latent: bfloat16 [32, 256, 512], P(('rep', 'blk', 'sect', 'sub')), parts along dimension 0, may hold values from -16 to 16
- cache_rope: bfloat16 [32, 64, 256], P(('rep', 'blk', 'sect', 'sub')), parts along dimension 0, may hold values from -4.5 to 4.5
- lengths: int32 [32], P('rep'), parts along dimension 0, may hold values from 64 to 256, as said below
- positions: int32 [64], P(('rep', 'blk')), parts along dimension 0, may hold values from 2048 to 4095
- value_weight: bfloat16 [128, 512, 128], P(('sect', 'sub')), may hold values from -0.25 to 0.25
Outputs:
- attended: bfloat16 [64, 128, 128], P(('rep', 'blk'), ('sect', 'sub')), parts along dimension 0
The draws below stay inside these ranges and needn't reach their ends.
There are 2 independent parts, one for each index of `rep`. The reference program is written for one: setup_inputs(seed, part) draws one part's arguments, and reference() takes and returns one part's arrays. A program takes and returns all parts, laid end to end along the dimension named above; an argument that names none is the same for every part. Nothing has to cross between parts.
Inputs may be any that keep to these rules, and one draw needn't show every extreme that they name: `lengths`: in every draw some block has all 256 slots valid.
All inputs are finite; a program needn't handle non-finite values.
Results may differ from the reference program's by a relative error of at most 0.0075.
Values may be sent and summed in bfloat16 or wider, within the bound.
A program may use at most 64 MiB of HBM per device.

```python
import math
import jax
import jax.numpy as jnp
from jax import lax

L = 512
R = 64
H = 128
DV = 128
T_DEV = 256
QUERIES = 32
BLOCKS = 16
CACHE = 4096


def joint_draw(key):
    cache_values = jnp.clip(jax.random.normal(jax.random.fold_in(key, 1), (BLOCKS, T_DEV, L), jnp.float32), -4.5, 4.5)
    query_values = jnp.clip(3.0 * jax.random.normal(jax.random.fold_in(key, 2), (QUERIES, H, L), jnp.float32), -18.0, 18.0)
    return (query_values, cache_values)


def draw_query_latent(key, part):
    return joint_draw(key)[0].astype(jnp.bfloat16)


def draw_cache_latent(key, part):
    return joint_draw(key)[1].astype(jnp.bfloat16)


def draw_query_rope(key, part):
    values = jnp.clip(3.0 * jax.random.normal(jax.random.fold_in(key, 8), (QUERIES, R, H), jnp.float32), -18.0, 18.0)
    return values.astype(jnp.bfloat16)


def draw_lengths(key, part):
    counts = jax.random.randint(jax.random.fold_in(key, 21), (BLOCKS,), T_DEV // 4, T_DEV + 1)
    fullest = jax.random.randint(jax.random.fold_in(key, 22), (), 0, BLOCKS)
    return jnp.where(jnp.arange(BLOCKS) == fullest, T_DEV, counts).astype(jnp.int32)


def touch_ends(result, own_key, least, high):
    index_at = [jax.random.randint(jax.random.fold_in(own_key, axis), (), 0, length) for axis, length in enumerate(result.shape)]
    longest = result.shape.index(max(result.shape))
    neighbour = index_at[:longest] + [(index_at[longest] + 1) % result.shape[longest]] + index_at[longest + 1:]
    return result.at[tuple(index_at)].set(least).at[tuple(neighbour)].set(high)


def block_scale(own_key, dims, split, low, high):
    loudness, own = 1.0, jax.random.fold_in(own_key, 6)
    for axis_at, shards_of in split:
        draws = jnp.exp(jax.random.uniform(jax.random.fold_in(own, axis_at), (shards_of,), jnp.float32, low / len(split), high / len(split)))
        loudness = loudness * jnp.repeat(draws, dims[axis_at] // shards_of).reshape([-1 if axis == axis_at else 1 for axis in range(len(dims))])
    return loudness


def bell_draw(own_key, extent, scale, limit, cuts=(), held_as=jnp.bfloat16):
    values = jax.random.normal(own_key, extent, jnp.float32) * scale
    if len(cuts) > 0:
        values = block_scale(own_key, extent, cuts, -0.22, 0.18) * values
    return jnp.clip(values, min=-limit, max=limit).astype(held_as)


def setup_inputs(seed: int = 0, part: int = 0) -> dict:
    seeds = jax.random.split(jax.random.key(seed), 8)
    own_keys = jax.random.split(jax.random.fold_in(seeds[7], part), 8)
    return {
        "query_latent": draw_query_latent(jax.random.fold_in(jax.random.fold_in(seeds[7], part), 71), part),
        "query_rope": draw_query_rope(jax.random.fold_in(jax.random.fold_in(seeds[7], part), 71), part),
        "cache_latent": draw_cache_latent(jax.random.fold_in(jax.random.fold_in(seeds[7], part), 71), part),
        "cache_rope": bell_draw(own_keys[3], (BLOCKS, R, T_DEV), 1.0, 4.5, ((0, 16),)),
        "lengths": draw_lengths(jax.random.fold_in(jax.random.fold_in(seeds[7], part), 71), part),
        "positions": touch_ends(jax.random.randint(own_keys[5], (QUERIES,), CACHE // 2, CACHE), jax.random.fold_in(own_keys[5], 1), CACHE // 2, CACHE - 1).astype(jnp.int32),
        "value_weight": bell_draw(seeds[6], (H, L, DV), L ** -0.5, 0.25, ((0, 4),)),
    }


lowest_score = -1e+30

def reference(query_latent, query_rope, cache_latent, cache_rope, lengths, positions, value_weight):
    score_scale = 1.0 / math.sqrt(L + R)
    flat_latent = cache_latent.reshape(CACHE, L)
    flat_rope = jnp.transpose(cache_rope, (1, 0, 2)).reshape(R, CACHE)
    places = jnp.arange(CACHE, dtype=jnp.int32)
    block_fill = jnp.repeat(lengths, T_DEV, total_repeat_length=CACHE)
    filled = places % T_DEV < block_fill
    wide_weight = value_weight.astype(jnp.float32)

    def one_query(inputs):
        latent_row, rope_row, position = inputs
        scores = lax.dot_general(latent_row, flat_latent, (((1,), (1,)), ((), ())), preferred_element_type=jnp.float32)
        scores = scores + jnp.dot(rope_row.T, flat_rope, preferred_element_type=jnp.float32)
        scores = scores * score_scale
        visible = (filled & (places <= position))[None, :]
        scores = jnp.where(visible, scores, lowest_score)
        top = lax.optimization_barrier(jnp.max(scores, axis=1, keepdims=True))
        weights = jnp.where(visible, jnp.exp(scores - top), 0.0)
        total = lax.optimization_barrier(jnp.sum(weights, axis=1, keepdims=True))
        mixed = jnp.dot(weights.astype(jnp.bfloat16), flat_latent, preferred_element_type=jnp.float32)
        latent = (mixed / total).astype(jnp.bfloat16)
        return jnp.einsum('hl,hld->hd', latent.astype(jnp.float32), wide_weight).astype(jnp.bfloat16)
    return lax.map(one_query, (query_latent, query_rope, positions))
```

```python
import functools
import math

import jax
import jax.numpy as jnp
from jax import lax
from jax.experimental import pallas as pl
from jax.experimental.pallas import tpu as pltpu
from jax.sharding import PartitionSpec as P

lowest_score = -1e30
LANES = 128
MESH = pl.DeviceIdType.MESH


def spread(column, width):
    return jnp.concatenate([column] * (width // LANES), axis=1)


def kernel(
    sizes, query_hbm, rope_q_ref, latent_hbm, rope_hbm, length_ref, position_ref, weight_hbm,
    out_ref,
    query_buf, rope_q_buf, latent_buf, rope_buf, weight_buf, place_buf,
    top_buf, sum_buf, acc_buf, send_buf, send_stat, recv_buf, recv_stat,
    local_sem, z_send, z_recv, pair_send, pair_recv, part_send, part_recv,
):
    blk_count, sect_count, sub_count, chunk_heads = sizes
    query_count, head_count, latent_width = query_hbm.shape
    rope_width = rope_q_ref.shape[1]
    token_count = latent_hbm.shape[1]
    own_heads = head_count // (sect_count * sub_count)
    group_rows = query_count * own_heads
    chunk_count = own_heads // chunk_heads
    chunk_rows = query_count * chunk_heads
    score_scale = 1.0 / math.sqrt(latent_width + rope_width)
    half = token_count // 2
    z = lax.axis_index("blk")
    x = lax.axis_index("sect")
    s = lax.axis_index("sub")

    barrier = pltpu.get_barrier_semaphore()

    def greet(device_id):
        pl.semaphore_signal(barrier, inc=1, device_id=device_id, device_id_type=MESH)

    for step in range(1, sub_count):
        greet({"sub": lax.rem(s + step, sub_count)})
    for step in range(1, sect_count):
        greet({"sect": lax.rem(x + step, sect_count)})

    @pl.when(z > 0)
    def _():
        greet({"blk": z - 1})

    @pl.when(z < blk_count - 1)
    def _():
        greet({"blk": z + 1})

    own_copies = [
        pltpu.make_async_copy(latent_hbm.at[0], latent_buf.at[z, s], local_sem.at[0]),
        pltpu.make_async_copy(rope_hbm.at[0], rope_buf.at[z, s], local_sem.at[1]),
    ]
    query_copies = [
        pltpu.make_async_copy(
            query_hbm.at[:, pl.ds(pl.multiple_of((g * sub_count + s) * own_heads, own_heads), own_heads), :],
            query_buf.at[g], local_sem.at[3 + g],
        )
        for g in range(sect_count)
    ]
    weight_copy = pltpu.make_async_copy(weight_hbm, weight_buf, local_sem.at[2])
    for copy in own_copies + query_copies:
        copy.start()

    neighbours = jnp.where(z > 0, 1, 0) + jnp.where(z < blk_count - 1, 1, 0)
    pl.semaphore_wait(barrier, sub_count - 1 + sect_count - 1 + neighbours)

    def piece(ref_pair, index):
        latent_ref, rope_ref = ref_pair
        if index == 0:
            return rope_ref
        return latent_ref.at[pl.ds((index - 1) * half, half)]

    def held(j, place):
        return latent_buf.at[j, place], rope_buf.at[j, place]

    def z_copy(source, j, index, way, target):
        return pltpu.make_async_remote_copy(
            src_ref=piece(source, index), dst_ref=piece(held(j, s), index),
            send_sem=z_send.at[way, j, index], recv_sem=z_recv.at[j, index],
            device_id={"blk": target}, device_id_type=MESH,
        )

    def pair_copy(source, j, index, step):
        return pltpu.make_async_remote_copy(
            src_ref=piece(source, index), dst_ref=piece(held(j, s), index),
            send_sem=pair_send.at[step - 1, j, index], recv_sem=pair_recv.at[step - 1, j, index],
            device_id={"sub": lax.rem(s + step, sub_count)}, device_id_type=MESH,
        )

    own = (latent_hbm.at[0], rope_hbm.at[0])
    pieces = range(3)
    for index in pieces:
        @pl.when(z < blk_count - 1)
        def _():
            z_copy(own, z, index, 0, z + 1).start()

        @pl.when(z > 0)
        def _():
            z_copy(own, z, index, 1, z - 1).start()

    for index in pieces:
        for step in range(1, sub_count):
            pair_copy(own, z, index, step).start()
    weight_copy.start()

    for q in range(query_count):
        turned = jnp.transpose(rope_q_ref[q].astype(jnp.float32)).astype(jnp.bfloat16)
        rope_q_buf[q] = turned
        place_buf[pl.ds(q * own_heads, own_heads), :] = jnp.full(
            (own_heads, token_count), position_ref[q], jnp.int32
        )
    top_buf[...] = jnp.full(top_buf.shape, lowest_score, jnp.float32)
    sum_buf[...] = jnp.zeros(sum_buf.shape, jnp.float32)
    acc_buf[...] = jnp.zeros(acc_buf.shape, jnp.float32)
    for copy in own_copies + query_copies:
        copy.wait()

    def absorb(j, place, g):
        root = (j * sect_count + x) * sub_count + place
        length = length_ref[root]
        block = latent_buf[j, place]
        heads_at = pl.multiple_of((g * sub_count + s) * own_heads, own_heads)
        rope_rows = rope_q_buf[:, pl.ds(heads_at, own_heads), :].reshape(group_rows, rope_width)
        scores = lax.dot_general(
            query_buf[g].reshape(group_rows, latent_width), block,
            (((1,), (1,)), ((), ())), preferred_element_type=jnp.float32,
        )
        scores = scores + jnp.dot(rope_rows, rope_buf[j, place], preferred_element_type=jnp.float32)
        offsets = lax.broadcasted_iota(jnp.int32, (group_rows, token_count), 1)
        visible = offsets < jnp.minimum(length, place_buf[...] - (root * token_count - 1))
        scores = jnp.where(visible, scores * score_scale, lowest_score)
        old_top = top_buf[g]
        new_top = jnp.maximum(old_top, jnp.max(scores, axis=1, keepdims=True))
        factor = jnp.exp(old_top - new_top)
        weights = jnp.where(visible, jnp.exp(scores - spread(new_top, token_count)), 0.0)
        sum_buf[g] = sum_buf[g] * factor + jnp.sum(weights, axis=1, keepdims=True)
        top_buf[g] = new_top
        acc_buf[g] = acc_buf[g] * spread(factor, latent_width) + jnp.dot(
            weights.astype(jnp.bfloat16), block, preferred_element_type=jnp.float32
        )

    def wait_pair(j, step):
        for index in pieces:
            pair_copy(held(j, s), j, index, step).wait_recv()

    def source_of(step):
        return lax.rem(s + sub_count - step, sub_count)

    def absorb_all(j):
        def over_groups(place):
            def one(g, carry):
                absorb(j, place, g)
                return carry
            lax.fori_loop(0, sect_count, one, 0)

        over_groups(s)
        for step in range(1, sub_count):
            wait_pair(j, step)
            over_groups(source_of(step))

    def pass_on(k):
        for index in pieces:
            for way in range(2):
                j = z - k if way == 0 else z + k
                target = z + 1 if way == 0 else z - 1
                here = j >= 0 if way == 0 else j < blk_count
                further = target < blk_count if way == 0 else target >= 0

                @pl.when(here)
                def _():
                    z_copy(held(j, s), j, index, way, z).wait_recv()

                    @pl.when(further)
                    def _():
                        z_copy(held(j, s), j, index, way, target).start()

                    for step in range(1, sub_count):
                        pair_copy(held(j, s), j, index, step).start()

    absorb_all(z)

    def one_step(k, carry):
        pass_on(k)

        def one_way(way, inner):
            j = z + (2 * way - 1) * k

            @pl.when((j >= 0) & (j < blk_count))
            def _():
                absorb_all(j)
            return inner
        lax.fori_loop(0, 2, one_way, 0)
        return carry

    lax.fori_loop(1, blk_count - 1, one_step, 0)

    if blk_count > 1:
        pass_on(blk_count - 1)
    at_end = ((z == 0) | (z == blk_count - 1)) & (blk_count > 1)
    last = jnp.where(z == 0, blk_count - 1, 0)

    def part_copies(step, c):
        target = {"sect": lax.rem(x + step, sect_count)}
        return [
            pltpu.make_async_remote_copy(
                src_ref=source.at[step - 1, c], dst_ref=landing.at[step - 1, c],
                send_sem=part_send.at[step - 1, c, i], recv_sem=part_recv.at[step - 1, c, i],
                device_id=target, device_id_type=MESH,
            )
            for i, (source, landing) in enumerate(((send_buf, recv_buf), (send_stat, recv_stat)))
        ]

    def rows_of(value, c):
        width = value.shape[-1]
        cut = value.reshape(query_count, own_heads, width)[:, c * chunk_heads:(c + 1) * chunk_heads, :]
        return cut.reshape(chunk_rows, width)

    for step in range(1, sect_count):
        g = lax.rem(x + step, sect_count)

        @pl.when(at_end)
        def _():
            absorb(last, s, g)
            for pair_step in range(1, sub_count):
                if step == 1:
                    wait_pair(last, pair_step)
                absorb(last, source_of(pair_step), g)

        for c in range(chunk_count):
            send_buf[step - 1, c] = rows_of(acc_buf[g], c).astype(jnp.bfloat16)
            send_stat[step - 1, c, 0:8] = jnp.transpose(rows_of(top_buf[g], c))[0:8]
            send_stat[step - 1, c, 8:16] = jnp.transpose(rows_of(sum_buf[g], c))[0:8]
            for copy in part_copies(step, c):
                copy.start()

    @pl.when(at_end)
    def _():
        absorb(last, s, x)
        for pair_step in range(1, sub_count):
            if sect_count == 1:
                wait_pair(last, pair_step)
            absorb(last, source_of(pair_step), x)

    weight_copy.wait()
    row_head = lax.rem(lax.broadcasted_iota(jnp.int32, (chunk_rows, weight_hbm.shape[2]), 0), chunk_heads)
    value_width = weight_hbm.shape[2]
    for c in range(chunk_count):
        tops = [rows_of(top_buf[x], c)]
        sums = [rows_of(sum_buf[x], c)]
        outs = [rows_of(acc_buf[x], c)]
        for step in range(1, sect_count):
            for copy in part_copies(step, c):
                copy.wait_recv()
            stat = recv_stat[step - 1, c]
            tops.append(jnp.transpose(jnp.broadcast_to(stat[0:1], (LANES, chunk_rows))))
            sums.append(jnp.transpose(jnp.broadcast_to(stat[8:9], (LANES, chunk_rows))))
            outs.append(recv_buf[step - 1, c].astype(jnp.float32))
        overall = functools.reduce(jnp.maximum, tops)
        factors = [jnp.exp(top - overall) for top in tops]
        total = sum(part * factor for part, factor in zip(sums, factors))
        latent = sum(
            part * spread(factor / total, latent_width) for part, factor in zip(outs, factors)
        ).astype(jnp.bfloat16)
        result = jnp.zeros((chunk_rows, value_width), jnp.float32)
        for h in range(0, chunk_heads, 2):
            pair = jnp.concatenate(
                [weight_buf[c * chunk_heads + h], weight_buf[c * chunk_heads + h + 1]], axis=1
            )
            both = jnp.dot(latent, pair, preferred_element_type=jnp.float32)
            result = jnp.where(row_head == h, both[:, :value_width], result)
            result = jnp.where(row_head == h + 1, both[:, value_width:], result)
        out_ref[:, c * chunk_heads:(c + 1) * chunk_heads, :] = result.reshape(
            query_count, chunk_heads, value_width
        ).astype(out_ref.dtype)

    for step in range(1, sect_count):
        for c in range(chunk_count):
            for copy in part_copies(step, c):
                copy.wait_send()

    def drain(j, carry):
        for index in pieces:
            @pl.when((j <= z) & (z < blk_count - 1))
            def _():
                z_copy(held(j, s), j, index, 0, z).wait_send()

            @pl.when((j >= z) & (z > 0))
            def _():
                z_copy(held(j, s), j, index, 1, z).wait_send()

            for step in range(1, sub_count):
                pair_copy(held(j, s), j, index, step).wait_send()
        return carry

    lax.fori_loop(0, blk_count, drain, 0)


def shards(query_latent, query_rope, cache_latent, cache_rope, lengths, positions, value_weight):
    query_count, head_count, latent_width = query_latent.shape
    rope_width = query_rope.shape[1]
    token_count = cache_latent.shape[1]
    blk_count, sect_count, sub_count = (lax.axis_size(name) for name in ("blk", "sect", "sub"))
    own_heads, _, value_width = value_weight.shape
    chunk_heads = min(16, own_heads)
    chunk_count = own_heads // chunk_heads
    chunk_rows = query_count * chunk_heads
    group_rows = query_count * own_heads
    peers = max(sect_count - 1, 1)
    pairs = max(sub_count - 1, 1)
    bf16, f32 = jnp.bfloat16, jnp.float32
    anywhere = pl.BlockSpec(memory_space=pl.ANY)
    vmem = pl.BlockSpec(memory_space=pltpu.VMEM)
    smem = pl.BlockSpec(memory_space=pltpu.SMEM)
    dma = pltpu.SemaphoreType.DMA
    return pl.pallas_call(
        functools.partial(kernel, (blk_count, sect_count, sub_count, chunk_heads)),
        out_shape=jax.ShapeDtypeStruct((query_count, own_heads, value_width), bf16),
        in_specs=[anywhere, vmem, anywhere, anywhere, smem, smem, anywhere],
        out_specs=vmem,
        scratch_shapes=[
            pltpu.VMEM((sect_count, query_count, own_heads, latent_width), bf16),
            pltpu.VMEM((query_count, head_count, rope_width), bf16),
            pltpu.VMEM((blk_count, sub_count, token_count, latent_width), bf16),
            pltpu.VMEM((blk_count, sub_count, rope_width, token_count), bf16),
            pltpu.VMEM((own_heads, latent_width, value_width), bf16),
            pltpu.VMEM((group_rows, token_count), jnp.int32),
            pltpu.VMEM((sect_count, group_rows, LANES), f32),
            pltpu.VMEM((sect_count, group_rows, LANES), f32),
            pltpu.VMEM((sect_count, group_rows, latent_width), f32),
            pltpu.VMEM((peers, chunk_count, chunk_rows, latent_width), bf16),
            pltpu.VMEM((peers, chunk_count, 16, chunk_rows), f32),
            pltpu.VMEM((peers, chunk_count, chunk_rows, latent_width), bf16),
            pltpu.VMEM((peers, chunk_count, 16, chunk_rows), f32),
            dma((3 + sect_count,)),
            dma((2, blk_count, 3)),
            dma((blk_count, 3)),
            dma((pairs, blk_count, 3)),
            dma((pairs, blk_count, 3)),
            dma((peers, chunk_count, 2)),
            dma((peers, chunk_count, 2)),
        ],
        compiler_params=pltpu.CompilerParams(
            collective_id=0, has_side_effects=True, vmem_limit_bytes=60 * 1024 * 1024
        ),
    )(query_latent, query_rope, cache_latent, cache_rope, lengths, positions, value_weight)


def solution(mesh):
    placed = (
        P(("rep", "blk"), None, None),
        P(("rep", "blk"), None, None),
        P(("rep", "blk", "sect", "sub"), None, None),
        P(("rep", "blk", "sect", "sub"), None, None),
        P("rep"),
        P(("rep", "blk")),
        P(("sect", "sub"), None, None),
    )
    return jax.shard_map(
        shards,
        mesh=mesh,
        in_specs=placed,
        out_specs=P(("rep", "blk"), ("sect", "sub"), None),
        check_vma=False,
    )
```

```python
import functools
import math

import jax
import jax.numpy as jnp
from jax import lax
from jax.experimental import pallas as pl
from jax.experimental.pallas import tpu as pltpu
from jax.sharding import PartitionSpec as P

lowest_score = -1e30
LANES = 128
MESH = pl.DeviceIdType.MESH


def spread(column, width):
    return jnp.concatenate([column] * (width // LANES), axis=1)


def kernel(
    sizes, query_hbm, rope_q_hbm, latent_hbm, rope_hbm, length_hbm, position_hbm, weight_hbm,
    out_ref,
    rope_q_ref, length_ref, position_ref, query_buf, rope_q_buf, latent_buf, rope_buf, weight_buf, place_buf,
    top_buf, sum_buf, acc_buf, send_buf, send_stat, recv_buf, recv_stat,
    local_sem, z_send, z_recv, pair_send, pair_recv, part_send, part_recv,
):
    blk_count, sect_count, sub_count, chunk_heads = sizes
    query_count, head_count, latent_width = query_hbm.shape
    rope_width = rope_q_hbm.shape[1]
    token_count = latent_hbm.shape[1]
    own_heads = head_count // (sect_count * sub_count)
    group_rows = query_count * own_heads
    chunk_count = own_heads // chunk_heads
    chunk_rows = query_count * chunk_heads
    score_scale = 1.0 / math.sqrt(latent_width + rope_width)
    half = token_count // 2
    z = lax.axis_index("blk")
    x = lax.axis_index("sect")
    s = lax.axis_index("sub")

    barrier = pltpu.get_barrier_semaphore()

    def greet(device_id):
        pl.semaphore_signal(barrier, inc=1, device_id=device_id, device_id_type=MESH)

    for step in range(1, sub_count):
        greet({"sub": lax.rem(s + step, sub_count)})
    for step in range(1, sect_count):
        greet({"sect": lax.rem(x + step, sect_count)})

    @pl.when(z > 0)
    def _():
        greet({"blk": z - 1})

    @pl.when(z < blk_count - 1)
    def _():
        greet({"blk": z + 1})

    own_copies = [
        pltpu.make_async_copy(latent_hbm.at[0], latent_buf.at[z, s], local_sem.at[0]),
        pltpu.make_async_copy(rope_hbm.at[0], rope_buf.at[z, s], local_sem.at[1]),
    ]
    query_copies = [
        pltpu.make_async_copy(
            query_hbm.at[:, pl.ds(pl.multiple_of((g * sub_count + s) * own_heads, own_heads), own_heads), :],
            query_buf.at[g], local_sem.at[3 + g],
        )
        for g in range(sect_count)
    ]
    weight_copy = pltpu.make_async_copy(weight_hbm, weight_buf, local_sem.at[2])
    small_copies = [
        pltpu.make_async_copy(source, landing, local_sem.at[3 + sect_count + i])
        for i, (source, landing) in enumerate(
            ((rope_q_hbm, rope_q_ref), (length_hbm, length_ref), (position_hbm, position_ref))
        )
    ]
    for copy in small_copies + own_copies + query_copies:
        copy.start()

    neighbours = jnp.where(z > 0, 1, 0) + jnp.where(z < blk_count - 1, 1, 0)
    pl.semaphore_wait(barrier, sub_count - 1 + sect_count - 1 + neighbours)

    def piece(ref_pair, index):
        latent_ref, rope_ref = ref_pair
        if index == 0:
            return rope_ref
        return latent_ref.at[pl.ds((index - 1) * half, half)]

    def held(j, place):
        return latent_buf.at[j, place], rope_buf.at[j, place]

    def z_copy(source, j, index, way, target):
        return pltpu.make_async_remote_copy(
            src_ref=piece(source, index), dst_ref=piece(held(j, s), index),
            send_sem=z_send.at[way, j, index], recv_sem=z_recv.at[j, index],
            device_id={"blk": target}, device_id_type=MESH,
        )

    def pair_copy(source, j, index, step):
        return pltpu.make_async_remote_copy(
            src_ref=piece(source, index), dst_ref=piece(held(j, s), index),
            send_sem=pair_send.at[step - 1, j, index], recv_sem=pair_recv.at[step - 1, j, index],
            device_id={"sub": lax.rem(s + step, sub_count)}, device_id_type=MESH,
        )

    own = (latent_hbm.at[0], rope_hbm.at[0])
    pieces = range(3)
    for index in pieces:
        @pl.when(z < blk_count - 1)
        def _():
            z_copy(own, z, index, 0, z + 1).start()

        @pl.when(z > 0)
        def _():
            z_copy(own, z, index, 1, z - 1).start()

    for index in pieces:
        for step in range(1, sub_count):
            pair_copy(own, z, index, step).start()
    weight_copy.start()

    for copy in small_copies:
        copy.wait()
    for q in range(query_count):
        turned = jnp.transpose(rope_q_ref[q].astype(jnp.float32)).astype(jnp.bfloat16)
        rope_q_buf[q] = turned
        place_buf[pl.ds(q * own_heads, own_heads), :] = jnp.full(
            (own_heads, token_count), position_ref[q], jnp.int32
        )
    top_buf[...] = jnp.full(top_buf.shape, lowest_score, jnp.float32)
    sum_buf[...] = jnp.zeros(sum_buf.shape, jnp.float32)
    acc_buf[...] = jnp.zeros(acc_buf.shape, jnp.float32)
    for copy in own_copies + query_copies:
        copy.wait()

    def absorb(j, place, g):
        root = (j * sect_count + x) * sub_count + place
        length = length_ref[root]
        block = latent_buf[j, place]
        heads_at = pl.multiple_of((g * sub_count + s) * own_heads, own_heads)
        rope_rows = rope_q_buf[:, pl.ds(heads_at, own_heads), :].reshape(group_rows, rope_width)
        scores = lax.dot_general(
            query_buf[g].reshape(group_rows, latent_width), block,
            (((1,), (1,)), ((), ())), preferred_element_type=jnp.float32,
        )
        scores = scores + jnp.dot(rope_rows, rope_buf[j, place], preferred_element_type=jnp.float32)
        offsets = lax.broadcasted_iota(jnp.int32, (group_rows, token_count), 1)
        visible = offsets < jnp.minimum(length, place_buf[...] - (root * token_count - 1))
        scores = jnp.where(visible, scores * score_scale, lowest_score)
        old_top = top_buf[g]
        new_top = jnp.maximum(old_top, jnp.max(scores, axis=1, keepdims=True))
        factor = jnp.exp(old_top - new_top)
        weights = jnp.where(visible, jnp.exp(scores - spread(new_top, token_count)), 0.0)
        sum_buf[g] = sum_buf[g] * factor + jnp.sum(weights, axis=1, keepdims=True)
        top_buf[g] = new_top
        acc_buf[g] = acc_buf[g] * spread(factor, latent_width) + jnp.dot(
            weights.astype(jnp.bfloat16), block, preferred_element_type=jnp.float32
        )

    def wait_pair(j, step):
        for index in pieces:
            pair_copy(held(j, s), j, index, step).wait_recv()

    def source_of(step):
        return lax.rem(s + sub_count - step, sub_count)

    def absorb_all(j):
        def over_groups(place):
            def one(g, carry):
                absorb(j, place, g)
                return carry
            lax.fori_loop(0, sect_count, one, 0)

        over_groups(s)
        for step in range(1, sub_count):
            wait_pair(j, step)
            over_groups(source_of(step))

    def pass_on(k):
        for index in pieces:
            for way in range(2):
                j = z - k if way == 0 else z + k
                target = z + 1 if way == 0 else z - 1
                here = j >= 0 if way == 0 else j < blk_count
                further = target < blk_count if way == 0 else target >= 0

                @pl.when(here)
                def _():
                    z_copy(held(j, s), j, index, way, z).wait_recv()

                    @pl.when(further)
                    def _():
                        z_copy(held(j, s), j, index, way, target).start()

                    for step in range(1, sub_count):
                        pair_copy(held(j, s), j, index, step).start()

    absorb_all(z)

    def one_step(k, carry):
        pass_on(k)

        def one_way(way, inner):
            j = z + (2 * way - 1) * k

            @pl.when((j >= 0) & (j < blk_count))
            def _():
                absorb_all(j)
            return inner
        lax.fori_loop(0, 2, one_way, 0)
        return carry

    lax.fori_loop(1, blk_count - 1, one_step, 0)

    if blk_count > 1:
        pass_on(blk_count - 1)
    at_end = ((z == 0) | (z == blk_count - 1)) & (blk_count > 1)
    last = jnp.where(z == 0, blk_count - 1, 0)

    def part_copies(step, c):
        target = {"sect": lax.rem(x + step, sect_count)}
        return [
            pltpu.make_async_remote_copy(
                src_ref=source.at[step - 1, c], dst_ref=landing.at[step - 1, c],
                send_sem=part_send.at[step - 1, c, i], recv_sem=part_recv.at[step - 1, c, i],
                device_id=target, device_id_type=MESH,
            )
            for i, (source, landing) in enumerate(((send_buf, recv_buf), (send_stat, recv_stat)))
        ]

    def rows_of(value, c):
        width = value.shape[-1]
        cut = value.reshape(query_count, own_heads, width)[:, c * chunk_heads:(c + 1) * chunk_heads, :]
        return cut.reshape(chunk_rows, width)

    for step in range(1, sect_count):
        g = lax.rem(x + step, sect_count)

        @pl.when(at_end)
        def _():
            absorb(last, s, g)
            for pair_step in range(1, sub_count):
                if step == 1:
                    wait_pair(last, pair_step)
                absorb(last, source_of(pair_step), g)

        for c in range(chunk_count):
            send_buf[step - 1, c] = rows_of(acc_buf[g], c).astype(jnp.bfloat16)
            send_stat[step - 1, c, 0:8] = jnp.transpose(rows_of(top_buf[g], c))[0:8]
            send_stat[step - 1, c, 8:16] = jnp.transpose(rows_of(sum_buf[g], c))[0:8]
            for copy in part_copies(step, c):
                copy.start()

    @pl.when(at_end)
    def _():
        absorb(last, s, x)
        for pair_step in range(1, sub_count):
            if sect_count == 1:
                wait_pair(last, pair_step)
            absorb(last, source_of(pair_step), x)

    weight_copy.wait()
    row_head = lax.rem(lax.broadcasted_iota(jnp.int32, (chunk_rows, weight_hbm.shape[2]), 0), chunk_heads)
    value_width = weight_hbm.shape[2]
    for c in range(chunk_count):
        tops = [rows_of(top_buf[x], c)]
        sums = [rows_of(sum_buf[x], c)]
        outs = [rows_of(acc_buf[x], c)]
        for step in range(1, sect_count):
            for copy in part_copies(step, c):
                copy.wait_recv()
            stat = recv_stat[step - 1, c]
            tops.append(jnp.transpose(jnp.broadcast_to(stat[0:1], (LANES, chunk_rows))))
            sums.append(jnp.transpose(jnp.broadcast_to(stat[8:9], (LANES, chunk_rows))))
            outs.append(recv_buf[step - 1, c].astype(jnp.float32))
        overall = functools.reduce(jnp.maximum, tops)
        factors = [jnp.exp(top - overall) for top in tops]
        total = sum(part * factor for part, factor in zip(sums, factors))
        latent = sum(
            part * spread(factor / total, latent_width) for part, factor in zip(outs, factors)
        ).astype(jnp.bfloat16)
        result = jnp.zeros((chunk_rows, value_width), jnp.float32)
        for h in range(0, chunk_heads, 2):
            pair = jnp.concatenate(
                [weight_buf[c * chunk_heads + h], weight_buf[c * chunk_heads + h + 1]], axis=1
            )
            both = jnp.dot(latent, pair, preferred_element_type=jnp.float32)
            result = jnp.where(row_head == h, both[:, :value_width], result)
            result = jnp.where(row_head == h + 1, both[:, value_width:], result)
        out_ref[:, c * chunk_heads:(c + 1) * chunk_heads, :] = result.reshape(
            query_count, chunk_heads, value_width
        ).astype(out_ref.dtype)

    for step in range(1, sect_count):
        for c in range(chunk_count):
            for copy in part_copies(step, c):
                copy.wait_send()

    def drain(j, carry):
        for index in pieces:
            @pl.when((j <= z) & (z < blk_count - 1))
            def _():
                z_copy(held(j, s), j, index, 0, z).wait_send()

            @pl.when((j >= z) & (z > 0))
            def _():
                z_copy(held(j, s), j, index, 1, z).wait_send()

            for step in range(1, sub_count):
                pair_copy(held(j, s), j, index, step).wait_send()
        return carry

    lax.fori_loop(0, blk_count, drain, 0)


def shards(query_latent, query_rope, cache_latent, cache_rope, lengths, positions, value_weight):
    query_count, head_count, latent_width = query_latent.shape
    rope_width = query_rope.shape[1]
    token_count = cache_latent.shape[1]
    blk_count, sect_count, sub_count = (lax.axis_size(name) for name in ("blk", "sect", "sub"))
    own_heads, _, value_width = value_weight.shape
    chunk_heads = min(16, own_heads)
    chunk_count = own_heads // chunk_heads
    chunk_rows = query_count * chunk_heads
    group_rows = query_count * own_heads
    peers = max(sect_count - 1, 1)
    pairs = max(sub_count - 1, 1)
    bf16, f32 = jnp.bfloat16, jnp.float32
    hbm = pl.BlockSpec(memory_space=pltpu.HBM)
    vmem = pl.BlockSpec(memory_space=pltpu.VMEM)
    dma = pltpu.SemaphoreType.DMA
    return pl.pallas_call(
        functools.partial(kernel, (blk_count, sect_count, sub_count, chunk_heads)),
        out_shape=jax.ShapeDtypeStruct((query_count, own_heads, value_width), bf16),
        in_specs=[hbm] * 7,
        out_specs=vmem,
        scratch_shapes=[
            pltpu.VMEM(query_rope.shape, bf16),
            pltpu.SMEM(lengths.shape, jnp.int32),
            pltpu.SMEM(positions.shape, jnp.int32),
            pltpu.VMEM((sect_count, query_count, own_heads, latent_width), bf16),
            pltpu.VMEM((query_count, head_count, rope_width), bf16),
            pltpu.VMEM((blk_count, sub_count, token_count, latent_width), bf16),
            pltpu.VMEM((blk_count, sub_count, rope_width, token_count), bf16),
            pltpu.VMEM((own_heads, latent_width, value_width), bf16),
            pltpu.VMEM((group_rows, token_count), jnp.int32),
            pltpu.VMEM((sect_count, group_rows, LANES), f32),
            pltpu.VMEM((sect_count, group_rows, LANES), f32),
            pltpu.VMEM((sect_count, group_rows, latent_width), f32),
            pltpu.VMEM((peers, chunk_count, chunk_rows, latent_width), bf16),
            pltpu.VMEM((peers, chunk_count, 16, chunk_rows), f32),
            pltpu.VMEM((peers, chunk_count, chunk_rows, latent_width), bf16),
            pltpu.VMEM((peers, chunk_count, 16, chunk_rows), f32),
            dma((6 + sect_count,)),
            dma((2, blk_count, 3)),
            dma((blk_count, 3)),
            dma((pairs, blk_count, 3)),
            dma((pairs, blk_count, 3)),
            dma((peers, chunk_count, 2)),
            dma((peers, chunk_count, 2)),
        ],
        compiler_params=pltpu.CompilerParams(
            collective_id=0, has_side_effects=True, vmem_limit_bytes=60 * 1024 * 1024
        ),
    )(query_latent, query_rope, cache_latent, cache_rope, lengths, positions, value_weight)


def solution(mesh):
    placed = (
        P(("rep", "blk"), None, None),
        P(("rep", "blk"), None, None),
        P(("rep", "blk", "sect", "sub"), None, None),
        P(("rep", "blk", "sect", "sub"), None, None),
        P("rep"),
        P(("rep", "blk")),
        P(("sect", "sub"), None, None),
    )
    return jax.shard_map(
        shards,
        mesh=mesh,
        in_specs=placed,
        out_specs=P(("rep", "blk"), ("sect", "sub"), None),
        check_vma=False,
    )
```
